256 devices in a mesh: wide: 32 (over x, y, core), narrow: 8 (over z).
Axes of the slice: x: 4, y: 4, z: 8, core: 2. Of those that a mesh axis runs over, the one named last changes fastest.
Arguments:
- gradient: float32 [2, 8192, 2048], P(None, 'wide', 'narrow'), may hold values from -6 to 6
- probe_modes: bfloat16 [4, 2, 256, 256], replicated, may hold values from -5 to 5
- mode_weights: bfloat16 [32, 8, 3, 4, 2, 256, 256], P('wide', 'narrow'), may hold values from -4 to 4
- offsets: int32 [32, 8, 3, 2], P('wide', 'narrow'), may hold values from -64 to 64, as said below
- counts: int32 [32, 8], P('wide', 'narrow'), may hold values from 1 to 3, as said below
Outputs:
- solution: float32 [2, 8192, 2048], P(None, 'wide', 'narrow')
- residual: float32 [2, 8192, 2048], P(None, 'wide', 'narrow')
The draws below stay inside these ranges and needn't reach their ends.
Inputs may be any that keep to these rules, and one draw needn't show every extreme that they name: `offsets`: each offset lies between -64 and 64; both ends are taken by some slot in every draw. `counts`: slots from a tile's count on are empty; some tile has all 3 slots live in every draw.
All inputs are finite; a program needn't handle non-finite values.
Results may differ from the reference program's by a relative error of at most 0.012.
Values sent between devices are 32-bit elements; how exact they have to be, the bound alone decides.
A program may use at most 128 MiB of HBM per device.

```python
import math
import jax
import jax.numpy as jnp
from jax import lax

W = 256
MODES = 4
FCAP = 3
STEPS = 2
HALO = 64
NX = 8192
NY = 2048
N_WIDE = 32
N_NARROW = 8


def draw_offsets(key, part):
    drawn = jax.random.randint(key, (N_WIDE, N_NARROW, FCAP, 2), -HALO, HALO + 1, dtype=jnp.int32)
    chosen = jax.random.randint(jax.random.fold_in(key, 7), (), 0, N_WIDE * N_NARROW, dtype=jnp.int32)
    tile_ids = jnp.arange(N_WIDE * N_NARROW, dtype=jnp.int32).reshape(N_WIDE, N_NARROW)[:, :, None, None]
    slot_ids = jnp.arange(FCAP, dtype=jnp.int32)[None, None, :, None]
    part_ids = jnp.arange(2, dtype=jnp.int32)[None, None, None, :]
    target = (tile_ids == chosen) & (slot_ids == 0)
    drawn = jnp.where(target & (part_ids == 0), HALO, drawn)
    drawn = jnp.where(target & (part_ids == 1), -HALO, drawn)
    return drawn


def draw_counts(key, part):
    drawn = jax.random.randint(key, (N_WIDE, N_NARROW), 1, FCAP + 1, dtype=jnp.int32)
    chosen = jax.random.randint(jax.random.fold_in(key, 11), (), 0, N_WIDE * N_NARROW, dtype=jnp.int32)
    tile_ids = jnp.arange(N_WIDE * N_NARROW, dtype=jnp.int32).reshape(N_WIDE, N_NARROW)
    return jnp.where(tile_ids == chosen, FCAP, drawn)


def block_scale(stream_key, extent, cuts, smallest, largest):
    level, own = 1.0, jax.random.fold_in(stream_key, 6)
    for axis_at, shards_of in cuts:
        steps = jnp.exp(jax.random.uniform(jax.random.fold_in(own, axis_at), (shards_of,), jnp.float32, smallest / len(cuts), largest / len(cuts)))
        level = level * jnp.repeat(steps, extent[axis_at] // shards_of).reshape([-1 if axis == axis_at else 1 for axis in range(len(extent))])
    return level


def noise(own_key, dims, spread, most, shards=(), kind=jnp.bfloat16):
    values = spread * jax.random.normal(own_key, dims, jnp.float32)
    if shards:
        values = values * block_scale(own_key, dims, shards, -0.22, 0.18)
    return jnp.clip(values, -most, most).astype(kind)


def setup_inputs(seed: int = 0) -> dict:
    splits = jax.random.split(jax.random.key(seed), 6)
    return {
        "gradient": noise(splits[0], (2, NX, NY), 1.0, 6.0, ((1, 32), (2, 8)), jnp.float32),
        "probe_modes": noise(splits[1], (MODES, 2, W, W), 0.7, 5.0),
        "mode_weights": noise(splits[2], (N_WIDE, N_NARROW, FCAP, MODES, 2, W, W), 0.5, 4.0, ((0, 32), (1, 8))),
        "offsets": draw_offsets(jax.random.fold_in(splits[5], 71), 0),
        "counts": draw_counts(jax.random.fold_in(splits[5], 71), 0),
    }


damping = 0.5

def dft_tables(length, sign):
    counter = jnp.arange(length, dtype=jnp.int32)
    phases = counter[:, None] * counter[None, :] % length
    angles = phases.astype(jnp.float32) * (2.0 * math.pi / length)
    factor = 1.0 / math.sqrt(length)
    real_part = jnp.cos(angles) * factor
    imag_part = -sign * jnp.sin(angles) * factor
    left_table = jnp.stack([jnp.stack([real_part, -imag_part]), jnp.stack([imag_part, real_part])]).astype(jnp.bfloat16)
    right_table = jnp.stack([jnp.stack([real_part, imag_part]), jnp.stack([-imag_part, real_part])]).astype(jnp.bfloat16)
    return (left_table, right_table)

def left_apply(table, values):
    return jnp.einsum('pqab,nqbc->npac', table.astype(jnp.float32), values.astype(jnp.float32), precision=lax.Precision.HIGHEST)

def right_apply(table, values):
    return jnp.einsum('nqac,qpcd->npad', values.astype(jnp.float32), table.astype(jnp.float32), precision=lax.Precision.HIGHEST)

def wave_pass(patches, probe_modes, weights, live_mask, forward_tables, inverse_tables):
    frames = patches.shape[0]
    modes = probe_modes.shape[0]
    length = probe_modes.shape[-1]
    probe_re = probe_modes[None, :, 0].astype(jnp.float32)
    probe_im = probe_modes[None, :, 1].astype(jnp.float32)
    patch_re = patches[:, None, 0]
    patch_im = patches[:, None, 1]
    exit_wave = jnp.stack([probe_re * patch_re - probe_im * patch_im, probe_re * patch_im + probe_im * patch_re], axis=2).astype(jnp.bfloat16)
    stacked = exit_wave.reshape(frames * modes, 2, length, length)
    partial_value = left_apply(forward_tables[0], stacked).astype(jnp.bfloat16)
    far_field = right_apply(forward_tables[1], partial_value).reshape(frames, modes, 2, length, length)
    weight_re = weights[:, :, 0].astype(jnp.float32)
    weight_im = weights[:, :, 1].astype(jnp.float32)
    projected = lax.optimization_barrier(jnp.sum(weight_re * far_field[:, :, 0] + weight_im * far_field[:, :, 1], axis=1)) * live_mask[:, None, None]
    weighted = jnp.stack([weight_re * projected[:, None], weight_im * projected[:, None]], axis=2).astype(jnp.bfloat16)
    partial_back = left_apply(inverse_tables[0], weighted.reshape(frames * modes, 2, length, length)).astype(jnp.bfloat16)
    near_field = right_apply(inverse_tables[1], partial_back).reshape(frames, modes, 2, length, length)
    near_re = near_field[:, :, 0]
    near_im = near_field[:, :, 1]
    contribution = jnp.stack([lax.optimization_barrier(jnp.sum(probe_re * near_re + probe_im * near_im, axis=1)), lax.optimization_barrier(jnp.sum(probe_re * near_im - probe_im * near_re, axis=1))], axis=1)
    return (contribution, projected)

def apply_operator(direction, probe_modes, mode_weights, offsets, counts, forward_tables, inverse_tables):
    padded = jnp.pad(direction, ((0, 0), (HALO, HALO), (HALO, HALO)))
    tile_total = N_WIDE * N_NARROW
    weights_flat = mode_weights.reshape(tile_total, FCAP, MODES, 2, W, W)
    offsets_flat = offsets.reshape(tile_total, FCAP, 2)
    counts_flat = counts.reshape(tile_total)
    slot_ids = jnp.arange(FCAP, dtype=jnp.int32)

    def visit(total, element):
        tile_number, tile_weights, tile_offsets, tile_count = element
        row_base = tile_number // N_NARROW * W + HALO
        col_base = tile_number % N_NARROW * W + HALO
        starts = []
        pieces = []
        for slot_index in range(FCAP):
            row_start = (row_base + tile_offsets[slot_index, 0]).astype(jnp.int32)
            col_start = (col_base + tile_offsets[slot_index, 1]).astype(jnp.int32)
            starts.append((row_start, col_start))
            pieces.append(lax.dynamic_slice(padded, (jnp.int32(0), row_start, col_start), (2, W, W)))
        live_mask = (slot_ids < tile_count).astype(jnp.float32)
        contribution, projected = wave_pass(jnp.stack(pieces), probe_modes, tile_weights, live_mask, forward_tables, inverse_tables)
        for slot_index in range(FCAP):
            row_start, col_start = starts[slot_index]
            region = lax.dynamic_slice(total, (jnp.int32(0), row_start, col_start), (2, W, W))
            total = lax.dynamic_update_slice(total, region + contribution[slot_index], (jnp.int32(0), row_start, col_start))
        return (total, None)
    total, unused = lax.scan(visit, jnp.zeros_like(padded), (jnp.arange(tile_total, dtype=jnp.int32), weights_flat, offsets_flat, counts_flat))
    return total[:, HALO:HALO + NX, HALO:HALO + NY] + damping * direction

def reference(gradient, probe_modes, mode_weights, offsets, counts):
    forward_tables = dft_tables(W, 1.0)
    inverse_tables = dft_tables(W, -1.0)
    solution = jnp.zeros_like(gradient)
    residual = gradient
    direction = gradient
    norm_now = jnp.sum(residual * residual)
    for iteration in range(STEPS):
        image = apply_operator(direction, probe_modes, mode_weights, offsets, counts, forward_tables, inverse_tables)
        alpha = norm_now / jnp.sum(direction * image)
        solution = solution + alpha * direction
        residual = residual - alpha * image
        if iteration + 1 < STEPS:
            norm_next = jnp.sum(residual * residual)
            direction = residual + norm_next / norm_now * direction
            norm_now = norm_next
    return (solution, residual)
```

```python
import functools
import math

import jax
import jax.numpy as jnp
import numpy as np
from jax import lax
from jax.experimental import pallas as pl
from jax.experimental.pallas import tpu as pltpu
from jax.sharding import PartitionSpec as P

W = 256
MODES = 4
FCAP = 3
HALO = 64
EXT = W + 2 * HALO
LANES = 128
DAMPING = 0.5
MESH = pl.DeviceIdType.MESH
F32 = jnp.float32
BF16 = jnp.bfloat16


def tables():
    counter = np.arange(W)
    angles = (counter[:, None] * counter[None, :] % W) * (2.0 * math.pi / W)
    re = np.cos(angles) / math.sqrt(W)
    s = np.sin(angles) / math.sqrt(W)
    ahead = np.block([[re, s], [-s, re]])
    back = np.block([[re, -s], [s, re]])
    return np.stack([ahead, back]).astype(jnp.bfloat16)


def kernel(
    wide,
    narrow,
    offs,
    counts,
    tab_hbm,
    grad_hbm,
    probe_hbm,
    weight_hbm,
    sol_ref,
    res_ref,
    grad,
    tab,
    probe,
    weight,
    ext,
    side,
    acc,
    acc_side,
    image,
    packs,
    rows_in,
    sides_in,
    patch,
    waves,
    parts,
    proj,
    pad,
    ar_src,
    ar_z,
    ar_w,
    load_sems,
    x_send,
    x_recv,
    ar_send,
    ar_recv,
):
    me_w, me_n = lax.axis_index("wide"), lax.axis_index("narrow")

    def dev(w, n):
        return (lax.rem(w, wide), lax.rem(n, narrow))

    up, down = me_w + wide - 1, me_w + 1
    left, right = me_n + narrow - 1, me_n + 1

    loads = [
        pltpu.make_async_copy(grad_hbm, grad, load_sems.at[0]),
        pltpu.make_async_copy(tab_hbm, tab, load_sems.at[1]),
        pltpu.make_async_copy(probe_hbm, probe, load_sems.at[2]),
        pltpu.make_async_copy(weight_hbm.at[0, 0], weight, load_sems.at[3]),
    ]
    for load in loads:
        load.start()

    barrier = pltpu.get_barrier_semaphore()

    def greet_w(i, c):
        pl.semaphore_signal(barrier, inc=1, device_id=dev(me_w + i, me_n), device_id_type=MESH)
        return c

    def greet_n(i, c):
        pl.semaphore_signal(barrier, inc=1, device_id=dev(me_w, me_n + i), device_id_type=MESH)
        return c

    for w in (up, down):
        for n in (left, right):
            pl.semaphore_signal(barrier, inc=1, device_id=dev(w, n), device_id_type=MESH)
    lax.fori_loop(1, narrow, greet_n, 0)
    lax.fori_loop(1, wide, greet_w, 0)

    lane = lax.broadcasted_iota(jnp.int32, (1, LANES), 1)
    low = lane < HALO

    def pack_halo(src, k):
        re0, im0 = src[0, :, :LANES], src[1, :, :LANES]
        re1, im1 = src[0, :, LANES:], src[1, :, LANES:]
        packs[k, 0, HALO : HALO + W, :] = jnp.where(low, re0, pltpu.roll(im0, HALO, 1))
        packs[k, 1, HALO : HALO + W, :] = jnp.where(low, pltpu.roll(im1, HALO, 1), re1)

    def exchange(k, row_up, row_down, corner_up, corner_down):
        mid = pl.ds(HALO, W)
        first, last = pl.ds(0, HALO), pl.ds(HALO + W, HALO)
        plan = [
            (packs.at[k, 0, mid], sides_in.at[k, 1, mid], (me_w, left)),
            (packs.at[k, 1, mid], sides_in.at[k, 0, mid], (me_w, right)),
            (row_up, rows_in.at[k, 1], (up, me_n)),
            (row_down, rows_in.at[k, 0], (down, me_n)),
            (packs.at[k, 0, corner_up], sides_in.at[k, 1, last], (up, left)),
            (packs.at[k, 1, corner_up], sides_in.at[k, 0, last], (up, right)),
            (packs.at[k, 0, corner_down], sides_in.at[k, 1, first], (down, left)),
            (packs.at[k, 1, corner_down], sides_in.at[k, 0, first], (down, right)),
        ]
        copies = [
            pltpu.make_async_remote_copy(
                src_ref=src,
                dst_ref=dst,
                send_sem=x_send.at[k, j],
                recv_sem=x_recv.at[k, j],
                device_id=dev(*where),
                device_id_type=MESH,
            )
            for j, (src, dst, where) in enumerate(plan)
        ]
        for copy in copies:
            copy.start()
        return copies

    def halo_exchange(k, src):
        return exchange(
            k,
            src.at[:, pl.ds(0, HALO)],
            src.at[:, pl.ds(W - HALO, HALO)],
            pl.ds(HALO, HALO),
            pl.ds(W, HALO),
        )

    def fold_exchange(k, step):
        return exchange(
            k,
            acc.at[step, :, pl.ds(0, HALO)],
            acc.at[step, :, pl.ds(HALO + W, HALO)],
            pl.ds(0, HALO),
            pl.ds(HALO + W, HALO),
        )

    has_up = (me_w > 0).astype(F32)
    has_down = (me_w < wide - 1).astype(F32)
    has_left = (me_n > 0).astype(F32)
    has_right = (me_n < narrow - 1).astype(F32)

    def unpacked_halo(k):
        scale = jnp.where(low, has_right, has_left)
        lf, rt = sides_in[k, 0], sides_in[k, 1]
        re = jnp.where(low, rt, lf) * scale
        im = pltpu.roll(jnp.where(low, lf, rt), HALO, 1) * scale
        return re, im

    def ar_start(a, value):
        ar_src[a, 0] = value
        ar_z[a, me_n] = value

        def send(i, c):
            pltpu.make_async_remote_copy(
                src_ref=ar_src.at[a, 0],
                dst_ref=ar_z.at[a, me_n],
                send_sem=ar_send.at[a, 0],
                recv_sem=ar_recv.at[a, 0],
                device_id=dev(me_w, me_n + i),
                device_id_type=MESH,
            ).start()
            return c

        lax.fori_loop(1, narrow, send, 0)

    def ar_middle(a):
        some = ar_z.at[a, pl.ds(0, narrow - 1)]
        pltpu.make_async_copy(some, some, ar_recv.at[a, 0]).wait()
        value = jnp.sum(ar_z[a], axis=0)
        ar_src[a, 1] = value
        ar_w[a, me_w] = value

        def send(i, c):
            pltpu.make_async_remote_copy(
                src_ref=ar_src.at[a, 1],
                dst_ref=ar_w.at[a, me_w],
                send_sem=ar_send.at[a, 1],
                recv_sem=ar_recv.at[a, 1],
                device_id=dev(me_w + i, me_n),
                device_id_type=MESH,
            ).start()
            return c

        lax.fori_loop(1, wide, send, 0)

    def ar_finish(a):
        some = ar_w.at[a, pl.ds(0, wide - 1)]
        pltpu.make_async_copy(some, some, ar_recv.at[a, 1]).wait()
        total = jnp.sum(ar_w[a], axis=0)
        total = jnp.sum(total, axis=1, keepdims=True)
        return total[0:1], total[1:2]

    def ar_drain(a):
        some = ar_z.at[a, pl.ds(0, narrow - 1)]
        pltpu.make_async_copy(some, some, ar_send.at[a, 0]).wait()
        some = ar_w.at[a, pl.ds(0, wide - 1)]
        pltpu.make_async_copy(some, some, ar_send.at[a, 1]).wait()

    def squares(x):
        s = jnp.sum(x * x, axis=0, keepdims=True)
        return s[:, :LANES] + s[:, LANES:]

    count = counts[0, 0]
    halves = (slice(0, LANES), slice(LANES, W))

    def forward(step):
        def frame(f, total):
            o0, o1 = offs[0, 0, f, 0], offs[0, 0, f, 1]
            own = (lane + o1 >= 0) & (lane + o1 < LANES)
            shift = lax.rem(LANES - o1, LANES)
            window = pl.ds(HALO + o0, W)
            for q in range(2):
                strip = side[step, q, window, :]
                a = jnp.where(lane < o1, strip, ext[step, q, 0, window, :])
                b = jnp.where(lane >= LANES + o1, strip, ext[step, q, 1, window, :])
                a, b = pltpu.roll(a, shift, 1), pltpu.roll(b, shift, 1)
                patch[q, :, :LANES] = jnp.where(own, a, b)
                patch[q, :, LANES:] = jnp.where(own, b, a)
            for m in range(MODES):
                pr, pi = probe[m, 0].astype(F32), probe[m, 1].astype(F32)
                xr, xi = patch[0], patch[1]
                waves[m, :W] = (pr * xr - pi * xi).astype(BF16)
                waves[m, W:] = (pr * xi + pi * xr).astype(BF16)
                part = jnp.dot(tab[0], waves[m], preferred_element_type=F32).astype(BF16)
                parts[m, :, :W] = part[:W]
                parts[m, :, W:] = part[W:]
                far = jnp.dot(parts[m], tab[1], preferred_element_type=F32)
                term = weight[f, m, 0].astype(F32) * far[:, :W] + weight[f, m, 1].astype(F32) * far[:, W:]
                if m == 0:
                    proj[f] = term
                else:
                    proj[f] += term
            live = (f < count).astype(F32)
            p = proj[f] * live
            proj[f] = p
            return total + squares(p)

        return lax.fori_loop(0, FCAP, frame, jnp.zeros((1, LANES), F32))

    def backward_frame(step, f):
        o0, o1 = offs[0, 0, f, 0], offs[0, 0, f, 1]
        p = proj[f]
        for m in range(MODES):
            waves[m, :W] = (weight[f, m, 0].astype(F32) * p).astype(BF16)
            waves[m, W:] = (weight[f, m, 1].astype(F32) * p).astype(BF16)
            part = jnp.dot(tab[1], waves[m], preferred_element_type=F32).astype(BF16)
            parts[m, :, :W] = part[:W]
            parts[m, :, W:] = part[W:]
            near = jnp.dot(parts[m], tab[0], preferred_element_type=F32)
            pr, pi = probe[m, 0].astype(F32), probe[m, 1].astype(F32)
            nr, ni = near[:, :W], near[:, W:]
            if m == 0:
                patch[0] = pr * nr + pi * ni
                patch[1] = pr * ni - pi * nr
            else:
                patch[0] += pr * nr + pi * ni
                patch[1] += pr * ni - pi * nr
        own = (lane - o1 >= 0) & (lane - o1 < LANES)
        shift = lax.rem(LANES + o1, LANES)
        window = pl.ds(HALO - o0, EXT)
        to_right, to_left = lane < o1, lane >= LANES + o1
        for q in range(2):
            a = pltpu.roll(patch[q, :, :LANES], shift, 1)
            b = pltpu.roll(patch[q, :, LANES:], shift, 1)
            pad[q, 0, 2 * HALO : 2 * HALO + W, :] = jnp.where(own, a, b)
            pad[q, 1, 2 * HALO : 2 * HALO + W, :] = jnp.where(own, b, a)
            a, b = pad[q, 0, window, :], pad[q, 1, window, :]
            acc[step, q, :, :LANES] += jnp.where(to_right, 0.0, a)
            acc[step, q, :, LANES:] += jnp.where(to_left, 0.0, b)
            acc_side[q] += jnp.where(to_right, a, jnp.where(to_left, b, 0.0))

    def backward(step):
        def frame(f, c):
            backward_frame(step, f)
            return c

        lax.fori_loop(1, FCAP, frame, 0)

    def pack_fold(k):
        re, im = acc_side[0], pltpu.roll(acc_side[1], HALO, 1)
        packs[k, 1] = jnp.where(low, re, im)
        packs[k, 0] = jnp.where(low, im, re)

    def fold_in(k, step):
        for q in range(2):
            for h in range(2):
                own = acc[step, q, HALO : HALO + W, halves[h]]
                image[q, :, halves[h]] = own + DAMPING * ext[step, q, h, HALO : HALO + W, :]
            image[q, :HALO, :] += rows_in[k, 0, q] * has_up
            image[q, W - HALO :, :] += rows_in[k, 1, q] * has_down
        lf, rt = sides_in[k, 0], sides_in[k, 1]
        for rows, piece, scale in (
            (slice(0, W), slice(HALO, HALO + W), 1.0),
            (slice(0, HALO), slice(0, HALO), has_up),
            (slice(W - HALO, W), slice(HALO + W, EXT), has_down),
        ):
            l, r = lf[piece] * (has_left * scale), rt[piece] * (has_right * scale)
            image[0, rows, :LANES] += jnp.where(low, l, 0.0)
            image[0, rows, LANES:] += jnp.where(low, 0.0, r)
            image[1, rows, :LANES] += jnp.where(low, pltpu.roll(l, HALO, 1), 0.0)
            image[1, rows, LANES:] += jnp.where(low, 0.0, pltpu.roll(r, HALO, 1))

    loads[0].wait()
    pack_halo(grad, 0)
    pl.semaphore_wait(barrier, wide + narrow + 2)
    x0 = halo_exchange(0, grad)

    pad[...] = jnp.zeros_like(pad)
    acc[...] = jnp.zeros_like(acc)
    acc_side[...] = jnp.zeros_like(acc_side)
    norm = jnp.zeros((1, LANES), F32)
    for q in range(2):
        for h in range(2):
            ext[0, q, h, HALO : HALO + W, :] = grad[q, :, halves[h]]
        norm += squares(grad[q])
    for load in loads[1:]:
        load.wait()

    for copy in x0:
        copy.wait_recv()
    ends = ((slice(0, HALO), 0, has_up), (slice(HALO + W, EXT), 1, has_down))
    for rows, e, scale in ends:
        for q in range(2):
            for h in range(2):
                ext[0, q, h, rows, :] = rows_in[0, e, q, :, halves[h]] * scale
    halo = unpacked_halo(0)
    for q in range(2):
        side[0, q] = halo[q]
        for rows, e, scale in ends:
            side[0, q, rows, :] = side[0, q, rows, :] * scale

    total = forward(0) + DAMPING * norm
    ar_start(0, jnp.concatenate([norm, total], axis=0))
    backward_frame(0, 0)
    ar_middle(0)
    backward(0)
    pack_fold(1)
    x1 = fold_exchange(1, 0)
    for copy in x1:
        copy.wait_recv()
    fold_in(1, 0)
    pack_halo(image, 2)
    x2 = halo_exchange(2, image)
    acc_side[...] = jnp.zeros_like(acc_side)

    norm0, curvature = ar_finish(0)
    alpha0 = norm0 / curvature
    norm = jnp.zeros((1, LANES), F32)
    for q in range(2):
        r = grad[q] - alpha0 * image[q]
        res_ref[q] = r
        norm += squares(r)
    ar_start(1, jnp.concatenate([norm, norm], axis=0))
    for copy in x2:
        copy.wait_recv()
    ar_middle(1)
    halo = unpacked_halo(2)
    for q in range(2):
        side[1, q] = side[0, q] - alpha0 * halo[q]
        for rows, e, scale in ends:
            for h in range(2):
                ext[1, q, h, rows, :] = ext[0, q, h, rows, :] - alpha0 * rows_in[2, e, q, :, halves[h]]
    norm1, _ = ar_finish(1)
    beta = norm1 / norm0
    norm = jnp.zeros((1, LANES), F32)
    for q in range(2):
        for h in range(2):
            d = res_ref[q, :, halves[h]] + beta * grad[q, :, halves[h]]
            ext[1, q, h, HALO : HALO + W, :] = d
            norm += jnp.sum(d * d, axis=0, keepdims=True)
        side[1, q] = side[1, q] + beta * side[0, q]
        for rows, e, scale in ends:
            for h in range(2):
                ext[1, q, h, rows, :] = (ext[1, q, h, rows, :] + beta * ext[0, q, h, rows, :]) * scale
            side[1, q, rows, :] = side[1, q, rows, :] * scale

    total = forward(1) + DAMPING * norm
    ar_start(2, jnp.concatenate([total, total], axis=0))
    backward_frame(1, 0)
    ar_middle(2)
    backward(1)
    pack_fold(3)
    x3 = fold_exchange(3, 1)
    for copy in x2:
        copy.wait_send()
    for copy in x3:
        copy.wait_recv()
    fold_in(3, 1)
    curvature, _ = ar_finish(2)
    alpha1 = norm1 / curvature
    for q in range(2):
        for h in range(2):
            sol_ref[q, :, halves[h]] = alpha0 * grad[q, :, halves[h]] + alpha1 * ext[1, q, h, HALO : HALO + W, :]
        res_ref[q] = res_ref[q] - alpha1 * image[q]

    for copy in x0 + x1 + x3:
        copy.wait_send()
    for a in range(3):
        ar_drain(a)


def solution(mesh):
    wide, narrow = mesh.shape["wide"], mesh.shape["narrow"]
    tab = tables()
    tile = jax.ShapeDtypeStruct((2, W, W), F32)
    hbm = pl.BlockSpec(memory_space=pl.ANY)
    smem = pl.BlockSpec(memory_space=pltpu.SMEM)
    vmem = pl.BlockSpec(memory_space=pltpu.VMEM)

    def local(gradient, probe_modes, mode_weights, offsets, counts):
        return pl.pallas_call(
            functools.partial(kernel, wide, narrow),
            out_shape=(tile, tile),
            in_specs=[smem, smem, hbm, hbm, hbm, hbm],
            out_specs=(vmem, vmem),
            scratch_shapes=[
                pltpu.VMEM((2, W, W), F32),
                pltpu.VMEM((2, 2 * W, 2 * W), BF16),
                pltpu.VMEM((MODES, 2, W, W), BF16),
                pltpu.VMEM((FCAP, MODES, 2, W, W), BF16),
                pltpu.VMEM((2, 2, 2, EXT, LANES), F32),
                pltpu.VMEM((2, 2, EXT, LANES), F32),
                pltpu.VMEM((2, 2, EXT, W), F32),
                pltpu.VMEM((2, EXT, LANES), F32),
                pltpu.VMEM((2, W, W), F32),
                pltpu.VMEM((4, 2, EXT, LANES), F32),
                pltpu.VMEM((4, 2, 2, HALO, W), F32),
                pltpu.VMEM((4, 2, EXT, LANES), F32),
                pltpu.VMEM((2, W, W), F32),
                pltpu.VMEM((MODES, 2 * W, W), BF16),
                pltpu.VMEM((MODES, W, 2 * W), BF16),
                pltpu.VMEM((FCAP, W, W), F32),
                pltpu.VMEM((2, 2, EXT + 2 * HALO, LANES), F32),
                pltpu.VMEM((3, 2, 2, LANES), F32),
                pltpu.VMEM((3, narrow, 2, LANES), F32),
                pltpu.VMEM((3, wide, 2, LANES), F32),
                pltpu.SemaphoreType.DMA((4,)),
                pltpu.SemaphoreType.DMA((4, 8)),
                pltpu.SemaphoreType.DMA((4, 8)),
                pltpu.SemaphoreType.DMA((3, 2)),
                pltpu.SemaphoreType.DMA((3, 2)),
            ],
            compiler_params=pltpu.CompilerParams(
                collective_id=0, has_side_effects=True, vmem_limit_bytes=60 * 1024 * 1024
            ),
        )(offsets, counts, jnp.asarray(tab), gradient, probe_modes, mode_weights)

    spec = P(None, "wide", "narrow")
    return jax.shard_map(
        local,
        mesh=mesh,
        in_specs=(
            spec,
            P(),
            P("wide", "narrow", None, None, None, None, None),
            P("wide", "narrow", None, None),
            P("wide", "narrow"),
        ),
        out_specs=(spec, spec),
        check_vma=False,
    )
```

```python
import functools
import math

import jax
import jax.numpy as jnp
import numpy as np
from jax import lax
from jax.experimental import pallas as pl
from jax.experimental.pallas import tpu as pltpu
from jax.sharding import PartitionSpec as P

W = 256
MODES = 4
FCAP = 3
HALO = 64
EXT = W + 2 * HALO
LANES = 128
DAMPING = 0.5
MESH = pl.DeviceIdType.MESH
F32 = jnp.float32
BF16 = jnp.bfloat16


def tables():
    counter = np.arange(W)
    angles = (counter[:, None] * counter[None, :] % W) * (2.0 * math.pi / W)
    re = np.cos(angles) / math.sqrt(W)
    s = np.sin(angles) / math.sqrt(W)
    ahead = np.block([[re, s], [-s, re]])
    back = np.block([[re, -s], [s, re]])
    return np.stack([ahead, back]).astype(jnp.bfloat16)


def kernel(
    wide,
    narrow,
    offs,
    counts,
    tab_hbm,
    grad_hbm,
    probe_hbm,
    weight_hbm,
    sol_ref,
    res_ref,
    grad,
    tab,
    probe,
    weight,
    ext,
    side,
    acc,
    acc_side,
    image,
    packs,
    rows_in,
    sides_in,
    patch,
    waves,
    parts,
    proj,
    pad,
    ar_src,
    ar_z,
    ar_w,
    load_sems,
    x_send,
    x_recv,
    ar_send,
    ar_recv,
):
    me_w, me_n = lax.axis_index("wide"), lax.axis_index("narrow")

    def dev(w, n):
        return (lax.rem(w, wide), lax.rem(n, narrow))

    up, down = me_w + wide - 1, me_w + 1
    left, right = me_n + narrow - 1, me_n + 1

    has_up, has_down = me_w > 0, me_w < wide - 1
    has_left, has_right = me_n > 0, me_n < narrow - 1

    loads = [
        pltpu.make_async_copy(grad_hbm, grad, load_sems.at[0]),
        pltpu.make_async_copy(tab_hbm, tab, load_sems.at[1]),
        pltpu.make_async_copy(probe_hbm, probe, load_sems.at[2]),
        pltpu.make_async_copy(weight_hbm.at[0, 0], weight, load_sems.at[3]),
    ]
    for load in loads:
        load.start()

    barrier = pltpu.get_barrier_semaphore()

    def greet_w(i, c):
        pl.semaphore_signal(barrier, inc=1, device_id=dev(me_w + i, me_n), device_id_type=MESH)
        return c

    def greet_n(i, c):
        pl.semaphore_signal(barrier, inc=1, device_id=dev(me_w, me_n + i), device_id_type=MESH)
        return c

    for w in (up, down):
        for n in (left, right):
            pl.semaphore_signal(barrier, inc=1, device_id=dev(w, n), device_id_type=MESH)
    lax.fori_loop(1, narrow, greet_n, 0)
    lax.fori_loop(1, wide, greet_w, 0)

    lane = lax.broadcasted_iota(jnp.int32, (1, LANES), 1)
    low = lane < HALO

    def pack_halo(src, k):
        re0, im0 = src[0, :, :LANES], src[1, :, :LANES]
        re1, im1 = src[0, :, LANES:], src[1, :, LANES:]
        packs[k, 0, HALO : HALO + W, :] = jnp.where(low, re0, pltpu.roll(im0, HALO, 1))
        packs[k, 1, HALO : HALO + W, :] = jnp.where(low, pltpu.roll(im1, HALO, 1), re1)

    def exchange(k, row_up, row_down, corner_up, corner_down):
        mid = pl.ds(HALO, W)
        first, last = pl.ds(0, HALO), pl.ds(HALO + W, HALO)
        plan = [
            (packs.at[k, 0, corner_up], sides_in.at[k, 1, last], (up, left), has_up & has_left, has_down & has_right),
            (packs.at[k, 1, corner_up], sides_in.at[k, 0, last], (up, right), has_up & has_right, has_down & has_left),
            (packs.at[k, 0, corner_down], sides_in.at[k, 1, first], (down, left), has_down & has_left, has_up & has_right),
            (packs.at[k, 1, corner_down], sides_in.at[k, 0, first], (down, right), has_down & has_right, has_up & has_left),
            (packs.at[k, 0, mid], sides_in.at[k, 1, mid], (me_w, left), has_left, has_right),
            (packs.at[k, 1, mid], sides_in.at[k, 0, mid], (me_w, right), has_right, has_left),
            (row_up, rows_in.at[k, 1], (up, me_n), has_up, has_down),
            (row_down, rows_in.at[k, 0], (down, me_n), has_down, has_up),
        ]
        copies = []
        for j, (src, dst, where, sends, receives) in enumerate(plan):
            copy = pltpu.make_async_remote_copy(
                src_ref=src,
                dst_ref=dst,
                send_sem=x_send.at[k, j],
                recv_sem=x_recv.at[k, j],
                device_id=dev(*where),
                device_id_type=MESH,
            )
            pl.when(sends)(copy.start)
            copies.append((copy, sends, receives))
        return copies

    def receive(copies):
        for copy, _, receives in copies:
            pl.when(receives)(copy.wait_recv)

    def sent(copies):
        for copy, sends, _ in copies:
            pl.when(sends)(copy.wait_send)

    def halo_exchange(k, src):
        return exchange(
            k,
            src.at[:, pl.ds(0, HALO)],
            src.at[:, pl.ds(W - HALO, HALO)],
            pl.ds(HALO, HALO),
            pl.ds(W, HALO),
        )

    def fold_exchange(k, step):
        return exchange(
            k,
            acc.at[step, :, pl.ds(0, HALO)],
            acc.at[step, :, pl.ds(HALO + W, HALO)],
            pl.ds(0, HALO),
            pl.ds(HALO + W, HALO),
        )

    def unpacked_halo(k):
        lf, rt = sides_in[k, 0], sides_in[k, 1]
        re = jnp.where(low, rt, lf)
        im = pltpu.roll(jnp.where(low, lf, rt), HALO, 1)
        return re, im

    def ar_start(a, value):
        ar_src[a, 0] = value
        ar_z[a, me_n] = value

        def send(i, c):
            pltpu.make_async_remote_copy(
                src_ref=ar_src.at[a, 0],
                dst_ref=ar_z.at[a, me_n],
                send_sem=ar_send.at[a, 0],
                recv_sem=ar_recv.at[a, 0],
                device_id=dev(me_w, me_n + i),
                device_id_type=MESH,
            ).start()
            return c

        lax.fori_loop(1, narrow, send, 0)

    def ar_middle(a):
        some = ar_z.at[a, pl.ds(0, narrow - 1)]
        pltpu.make_async_copy(some, some, ar_recv.at[a, 0]).wait()
        value = jnp.sum(ar_z[a], axis=0)
        ar_src[a, 1] = value
        ar_w[a, me_w] = value

        def send(i, c):
            pltpu.make_async_remote_copy(
                src_ref=ar_src.at[a, 1],
                dst_ref=ar_w.at[a, me_w],
                send_sem=ar_send.at[a, 1],
                recv_sem=ar_recv.at[a, 1],
                device_id=dev(me_w + i, me_n),
                device_id_type=MESH,
            ).start()
            return c

        lax.fori_loop(1, wide, send, 0)

    def ar_finish(a):
        some = ar_w.at[a, pl.ds(0, wide - 1)]
        pltpu.make_async_copy(some, some, ar_recv.at[a, 1]).wait()
        total = jnp.sum(ar_w[a], axis=0)
        total = jnp.sum(total, axis=1, keepdims=True)
        return total[0:1], total[1:2]

    def ar_drain(a):
        some = ar_z.at[a, pl.ds(0, narrow - 1)]
        pltpu.make_async_copy(some, some, ar_send.at[a, 0]).wait()
        some = ar_w.at[a, pl.ds(0, wide - 1)]
        pltpu.make_async_copy(some, some, ar_send.at[a, 1]).wait()

    def squares(x):
        s = jnp.sum(x * x, axis=0, keepdims=True)
        return s[:, :LANES] + s[:, LANES:]

    count = counts[0, 0]
    halves = (slice(0, LANES), slice(LANES, W))

    def load_patch(step, f):
        o0, o1 = offs[0, 0, 0, f], offs[0, 0, 1, f]
        own = (lane + o1 >= 0) & (lane + o1 < LANES)
        shift = lax.rem(LANES - o1, LANES)
        window = pl.ds(HALO + o0, W)
        for q in range(2):
            strip = side[step, q, window, :]
            a = jnp.where(lane < o1, strip, ext[step, q, 0, window, :])
            b = jnp.where(lane >= LANES + o1, strip, ext[step, q, 1, window, :])
            a, b = pltpu.roll(a, shift, 1), pltpu.roll(b, shift, 1)
            patch[q, :, :LANES] = jnp.where(own, a, b)
            patch[q, :, LANES:] = jnp.where(own, b, a)

    def exit_wave(m):
        pr, pi = probe[m, 0].astype(F32), probe[m, 1].astype(F32)
        xr, xi = patch[0], patch[1]
        waves[m, :W] = (pr * xr - pi * xi).astype(BF16)
        waves[m, W:] = (pr * xi + pi * xr).astype(BF16)

    def weigh(step, f, m):
        p = proj[step, f]
        waves[m, :W] = (weight[f, m, 0].astype(F32) * p).astype(BF16)
        waves[m, W:] = (weight[f, m, 1].astype(F32) * p).astype(BF16)

    def transform(left_table, right_table, refill):
        for m in range(MODES):
            part = jnp.dot(tab[left_table], waves[m], preferred_element_type=F32).astype(BF16)
            parts[m * W : (m + 1) * W, :W] = part[:W]
            parts[m * W : (m + 1) * W, W:] = part[W:]
            refill(m)
        return jnp.dot(parts[...], tab[right_table], preferred_element_type=F32)

    def forward(step):
        load_patch(step, 0)
        for m in range(MODES):
            exit_wave(m)

        def frame(f, total):
            load_patch(step, jnp.minimum(f + 1, FCAP - 1))
            far = transform(0, 1, exit_wave)
            p = jnp.zeros((W, W), F32)
            for m in range(MODES):
                one = far[m * W : (m + 1) * W]
                p += weight[f, m, 0].astype(F32) * one[:, :W] + weight[f, m, 1].astype(F32) * one[:, W:]
            p = p * (f < count).astype(F32)
            proj[step, f] = p
            return total + squares(p)

        return lax.fori_loop(0, FCAP, frame, jnp.zeros((1, LANES), F32))

    def spread(step, f):
        o0, o1 = offs[0, 0, 0, f], offs[0, 0, 1, f]
        own = (lane - o1 >= 0) & (lane - o1 < LANES)
        shift = lax.rem(LANES + o1, LANES)
        window = pl.ds(HALO - o0, EXT)
        to_right, to_left = lane < o1, lane >= LANES + o1
        for q in range(2):
            a = pltpu.roll(patch[q, :, :LANES], shift, 1)
            b = pltpu.roll(patch[q, :, LANES:], shift, 1)
            pad[q, 0, 2 * HALO : 2 * HALO + W, :] = jnp.where(own, a, b)
            pad[q, 1, 2 * HALO : 2 * HALO + W, :] = jnp.where(own, b, a)
            a, b = pad[q, 0, window, :], pad[q, 1, window, :]
            acc[step, q, :, :LANES] += jnp.where(to_right, 0.0, a)
            acc[step, q, :, LANES:] += jnp.where(to_left, 0.0, b)
            acc_side[q] += jnp.where(to_right, a, jnp.where(to_left, b, 0.0))

    def backward(step):
        for m in range(MODES):
            weigh(step, 0, m)
        patch[...] = jnp.zeros_like(patch)

        def frame(f, c):
            spread(step, jnp.maximum(f - 1, 0))
            near = transform(1, 0, functools.partial(weigh, step, jnp.minimum(f + 1, FCAP - 1)))
            re, im = jnp.zeros((W, W), F32), jnp.zeros((W, W), F32)
            for m in range(MODES):
                pr, pi = probe[m, 0].astype(F32), probe[m, 1].astype(F32)
                nr, ni = near[m * W : (m + 1) * W, :W], near[m * W : (m + 1) * W, W:]
                re += pr * nr + pi * ni
                im += pr * ni - pi * nr
            patch[0], patch[1] = re, im
            return c

        lax.fori_loop(0, FCAP, frame, 0)
        ar_middle(2 * step)
        spread(step, FCAP - 1)

    def pack_fold(k):
        re, im = acc_side[0], pltpu.roll(acc_side[1], HALO, 1)
        packs[k, 1] = jnp.where(low, re, im)
        packs[k, 0] = jnp.where(low, im, re)

    def fold_in(k, step):
        for q in range(2):
            for h in range(2):
                own = acc[step, q, HALO : HALO + W, halves[h]]
                image[q, :, halves[h]] = own + DAMPING * ext[step, q, h, HALO : HALO + W, :]
            image[q, :HALO, :] += rows_in[k, 0, q]
            image[q, W - HALO :, :] += rows_in[k, 1, q]
        lf, rt = sides_in[k, 0], sides_in[k, 1]
        for rows, piece in (
            (slice(0, W), slice(HALO, HALO + W)),
            (slice(0, HALO), slice(0, HALO)),
            (slice(W - HALO, W), slice(HALO + W, EXT)),
        ):
            l, r = lf[piece], rt[piece]
            image[0, rows, :LANES] += jnp.where(low, l, 0.0)
            image[0, rows, LANES:] += jnp.where(low, 0.0, r)
            image[1, rows, :LANES] += jnp.where(low, pltpu.roll(l, HALO, 1), 0.0)
            image[1, rows, LANES:] += jnp.where(low, 0.0, pltpu.roll(r, HALO, 1))

    loads[0].wait()
    pack_halo(grad, 0)
    pl.semaphore_wait(barrier, wide + narrow + 2)
    x0 = halo_exchange(0, grad)

    def no_rows(e, rows):
        rows_in[:, e] = jnp.zeros_like(rows_in[:, e])
        sides_in[:, :, rows, :] = jnp.zeros_like(sides_in[:, :, rows, :])

    def no_columns(e):
        sides_in[:, e] = jnp.zeros_like(sides_in[:, e])

    pl.when(~has_up)(lambda: no_rows(0, slice(0, HALO)))
    pl.when(~has_down)(lambda: no_rows(1, slice(HALO + W, EXT)))
    pl.when(~has_left)(lambda: no_columns(0))
    pl.when(~has_right)(lambda: no_columns(1))
    pad[...] = jnp.zeros_like(pad)
    acc[...] = jnp.zeros_like(acc)
    acc_side[...] = jnp.zeros_like(acc_side)
    norm = jnp.zeros((1, LANES), F32)
    for q in range(2):
        for h in range(2):
            ext[0, q, h, HALO : HALO + W, :] = grad[q, :, halves[h]]
        norm += squares(grad[q])
    for load in loads[1:]:
        load.wait()

    receive(x0)
    ends = ((slice(0, HALO), 0), (slice(HALO + W, EXT), 1))
    for rows, e in ends:
        for q in range(2):
            for h in range(2):
                ext[0, q, h, rows, :] = rows_in[0, e, q, :, halves[h]]
    halo = unpacked_halo(0)
    for q in range(2):
        side[0, q] = halo[q]

    total = forward(0) + DAMPING * norm
    ar_start(0, jnp.concatenate([norm, total], axis=0))
    backward(0)
    pack_fold(1)
    x1 = fold_exchange(1, 0)
    receive(x1)
    fold_in(1, 0)
    pack_halo(image, 2)
    x2 = halo_exchange(2, image)
    acc_side[...] = jnp.zeros_like(acc_side)

    norm0, curvature = ar_finish(0)
    alpha0 = norm0 / curvature
    norm = jnp.zeros((1, LANES), F32)
    for q in range(2):
        for h in range(2):
            r = grad[q, :, halves[h]] - alpha0 * image[q, :, halves[h]]
            ext[1, q, h, HALO : HALO + W, :] = r
            res_ref[q, :, halves[h]] = r
            norm += jnp.sum(r * r, axis=0, keepdims=True)
    ar_start(1, jnp.concatenate([norm, norm], axis=0))
    ar_middle(1)
    receive(x2)
    halo = unpacked_halo(2)
    for q in range(2):
        side[1, q] = side[0, q] - alpha0 * halo[q]
        for rows, e in ends:
            for h in range(2):
                ext[1, q, h, rows, :] = ext[0, q, h, rows, :] - alpha0 * rows_in[2, e, q, :, halves[h]]

    forward(1)
    norm1, _ = ar_finish(1)
    beta = norm1 / norm0
    norm = jnp.zeros((1, LANES), F32)
    total = jnp.zeros((1, LANES), F32)
    for f in range(FCAP):
        p = proj[1, f] + beta * proj[0, f]
        proj[1, f] = p
        total += squares(p)
    for q in range(2):
        for h in range(2):
            d = ext[1, q, h, HALO : HALO + W, :] + beta * grad[q, :, halves[h]]
            ext[1, q, h, HALO : HALO + W, :] = d
            norm += jnp.sum(d * d, axis=0, keepdims=True)
    total += DAMPING * norm
    ar_start(2, jnp.concatenate([total, total], axis=0))
    backward(1)
    pack_fold(3)
    x3 = fold_exchange(3, 1)
    sent(x2)
    receive(x3)
    fold_in(3, 1)
    curvature, _ = ar_finish(2)
    alpha1 = norm1 / curvature
    for q in range(2):
        for h in range(2):
            sol_ref[q, :, halves[h]] = alpha0 * grad[q, :, halves[h]] + alpha1 * ext[1, q, h, HALO : HALO + W, :]
        res_ref[q] = res_ref[q] - alpha1 * image[q]

    sent(x0 + x1 + x3)
    for a in range(3):
        ar_drain(a)


def copy_kernel(a, b, x, y, buffers, in_sems, out_sems):
    pairs = [(a.at[0], x.at[0]), (a.at[1], x.at[1]), (b.at[0], y.at[0]), (b.at[1], y.at[1])]
    ins = [pltpu.make_async_copy(src, buffers.at[i], in_sems.at[i]) for i, (src, _) in enumerate(pairs)]
    outs = [pltpu.make_async_copy(buffers.at[i], dst, out_sems.at[i]) for i, (_, dst) in enumerate(pairs)]
    for copy in ins:
        copy.start()
    for i, copy in enumerate(outs):
        ins[i].wait()
        copy.start()
    for copy in outs:
        copy.wait()


def solution(mesh):
    wide, narrow = mesh.shape["wide"], mesh.shape["narrow"]
    tab = tables()
    tile = jax.ShapeDtypeStruct((2, W, W), F32)
    hbm = pl.BlockSpec(memory_space=pl.ANY)
    smem = pl.BlockSpec(memory_space=pltpu.SMEM)
    vmem = pl.BlockSpec(memory_space=pltpu.VMEM)

    def local(gradient, probe_modes, mode_weights, offsets, counts):
        results = pl.pallas_call(
            functools.partial(kernel, wide, narrow),
            out_shape=(tile, tile),
            in_specs=[smem, smem, hbm, hbm, hbm, hbm],
            out_specs=(vmem, vmem),
            scratch_shapes=[
                pltpu.VMEM((2, W, W), F32),
                pltpu.VMEM((2, 2 * W, 2 * W), BF16),
                pltpu.VMEM((MODES, 2, W, W), BF16),
                pltpu.VMEM((FCAP, MODES, 2, W, W), BF16),
                pltpu.VMEM((2, 2, 2, EXT, LANES), F32),
                pltpu.VMEM((2, 2, EXT, LANES), F32),
                pltpu.VMEM((2, 2, EXT, W), F32),
                pltpu.VMEM((2, EXT, LANES), F32),
                pltpu.VMEM((2, W, W), F32),
                pltpu.VMEM((4, 2, EXT, LANES), F32),
                pltpu.VMEM((4, 2, 2, HALO, W), F32),
                pltpu.VMEM((4, 2, EXT, LANES), F32),
                pltpu.VMEM((2, W, W), F32),
                pltpu.VMEM((MODES, 2 * W, W), BF16),
                pltpu.VMEM((MODES * W, 2 * W), BF16),
                pltpu.VMEM((2, FCAP, W, W), F32),
                pltpu.VMEM((2, 2, EXT + 2 * HALO, LANES), F32),
                pltpu.VMEM((3, 2, 2, LANES), F32),
                pltpu.VMEM((3, narrow, 2, LANES), F32),
                pltpu.VMEM((3, wide, 2, LANES), F32),
                pltpu.SemaphoreType.DMA((4,)),
                pltpu.SemaphoreType.DMA((4, 8)),
                pltpu.SemaphoreType.DMA((4, 8)),
                pltpu.SemaphoreType.DMA((3, 2)),
                pltpu.SemaphoreType.DMA((3, 2)),
            ],
            compiler_params=pltpu.CompilerParams(
                collective_id=0, has_side_effects=True, vmem_limit_bytes=60 * 1024 * 1024
            ),
        )(jnp.swapaxes(offsets, 2, 3), counts, jnp.asarray(tab), gradient, probe_modes, mode_weights)
        return pl.pallas_call(
            copy_kernel,
            out_shape=(tile, tile),
            in_specs=[hbm, hbm],
            out_specs=(hbm, hbm),
            scratch_shapes=[
                pltpu.VMEM((4, W, W), F32),
                pltpu.SemaphoreType.DMA((4,)),
                pltpu.SemaphoreType.DMA((4,)),
            ],
            compiler_params=pltpu.CompilerParams(vmem_limit_bytes=60 * 1024 * 1024),
        )(*results)

    spec = P(None, "wide", "narrow")
    return jax.shard_map(
        local,
        mesh=mesh,
        in_specs=(
            spec,
            P(),
            P("wide", "narrow", None, None, None, None, None),
            P("wide", "narrow", None, None),
            P("wide", "narrow"),
        ),
        out_specs=(spec, spec),
        check_vma=False,
    )
```

```python
import functools
import math

import jax
import jax.numpy as jnp
import numpy as np
from jax import lax
from jax.experimental import pallas as pl
from jax.experimental.pallas import tpu as pltpu
from jax.sharding import PartitionSpec as P

W = 256
MODES = 4
FCAP = 3
HALO = 64
EXT = W + 2 * HALO
LANES = 128
DAMPING = 0.5
MESH = pl.DeviceIdType.MESH
F32 = jnp.float32
BF16 = jnp.bfloat16


def tables():
    counter = np.arange(W)
    angles = (counter[:, None] * counter[None, :] % W) * (2.0 * math.pi / W)
    re = np.cos(angles) / math.sqrt(W)
    s = np.sin(angles) / math.sqrt(W)
    ahead = np.block([[re, s], [-s, re]])
    back = np.block([[re, -s], [s, re]])
    return np.stack([ahead, back]).astype(jnp.bfloat16)


def kernel(
    wide,
    narrow,
    offs,
    counts,
    tab_hbm,
    grad_hbm,
    probe_hbm,
    weight_hbm,
    sol_ref,
    res_ref,
    grad,
    tab,
    probe,
    weight,
    ext,
    side,
    acc,
    acc_side,
    image,
    packs,
    rows_in,
    sides_in,
    patch,
    waves,
    parts,
    proj,
    pad,
    ar_src,
    ar_z,
    ar_w,
    load_sems,
    x_send,
    x_recv,
    ar_send,
    ar_recv,
):
    me_w, me_n = lax.axis_index("wide"), lax.axis_index("narrow")

    def dev(w, n):
        return (lax.rem(w, wide), lax.rem(n, narrow))

    up, down = me_w + wide - 1, me_w + 1
    left, right = me_n + narrow - 1, me_n + 1

    has_up, has_down = me_w > 0, me_w < wide - 1
    has_left, has_right = me_n > 0, me_n < narrow - 1

    loads = [
        pltpu.make_async_copy(grad_hbm, grad, load_sems.at[0]),
        pltpu.make_async_copy(tab_hbm, tab, load_sems.at[1]),
        pltpu.make_async_copy(probe_hbm, probe, load_sems.at[2]),
        pltpu.make_async_copy(weight_hbm.at[0, 0], weight, load_sems.at[3]),
    ]
    for load in loads:
        load.start()

    barrier = pltpu.get_barrier_semaphore()

    def greet_w(i, c):
        pl.semaphore_signal(barrier, inc=1, device_id=dev(me_w + i, me_n), device_id_type=MESH)
        return c

    def greet_n(i, c):
        pl.semaphore_signal(barrier, inc=1, device_id=dev(me_w, me_n + i), device_id_type=MESH)
        return c

    for w in (up, down):
        for n in (left, right):
            pl.semaphore_signal(barrier, inc=1, device_id=dev(w, n), device_id_type=MESH)
    lax.fori_loop(1, narrow, greet_n, 0)
    lax.fori_loop(1, wide, greet_w, 0)

    lane = lax.broadcasted_iota(jnp.int32, (1, LANES), 1)
    low = lane < HALO

    def pack_halo(src, k):
        re0, im0 = src[0, :, :LANES], src[1, :, :LANES]
        re1, im1 = src[0, :, LANES:], src[1, :, LANES:]
        packs[k, 0, HALO : HALO + W, :] = jnp.where(low, re0, pltpu.roll(im0, HALO, 1))
        packs[k, 1, HALO : HALO + W, :] = jnp.where(low, pltpu.roll(im1, HALO, 1), re1)

    def exchange(k, row_up, row_down, corner_up, corner_down):
        mid = pl.ds(HALO, W)
        first, last = pl.ds(0, HALO), pl.ds(HALO + W, HALO)
        plan = [
            (packs.at[k, 0, corner_up], sides_in.at[k, 1, last], (up, left), has_up & has_left, has_down & has_right),
            (packs.at[k, 1, corner_up], sides_in.at[k, 0, last], (up, right), has_up & has_right, has_down & has_left),
            (packs.at[k, 0, corner_down], sides_in.at[k, 1, first], (down, left), has_down & has_left, has_up & has_right),
            (packs.at[k, 1, corner_down], sides_in.at[k, 0, first], (down, right), has_down & has_right, has_up & has_left),
            (packs.at[k, 0, mid], sides_in.at[k, 1, mid], (me_w, left), has_left, has_right),
            (packs.at[k, 1, mid], sides_in.at[k, 0, mid], (me_w, right), has_right, has_left),
            (row_up, rows_in.at[k, 1], (up, me_n), has_up, has_down),
            (row_down, rows_in.at[k, 0], (down, me_n), has_down, has_up),
        ]
        copies = []
        for j, (src, dst, where, sends, receives) in enumerate(plan):
            copy = pltpu.make_async_remote_copy(
                src_ref=src,
                dst_ref=dst,
                send_sem=x_send.at[k, j],
                recv_sem=x_recv.at[k, j],
                device_id=dev(*where),
                device_id_type=MESH,
            )
            pl.when(sends)(copy.start)
            copies.append((copy, sends, receives))
        return copies

    def receive(copies):
        for copy, _, receives in copies:
            pl.when(receives)(copy.wait_recv)

    def sent(copies):
        for copy, sends, _ in copies:
            pl.when(sends)(copy.wait_send)

    def halo_exchange(k, src):
        return exchange(
            k,
            src.at[:, pl.ds(0, HALO)],
            src.at[:, pl.ds(W - HALO, HALO)],
            pl.ds(HALO, HALO),
            pl.ds(W, HALO),
        )

    def fold_exchange(k, step):
        return exchange(
            k,
            acc.at[step, :, pl.ds(0, HALO)],
            acc.at[step, :, pl.ds(HALO + W, HALO)],
            pl.ds(0, HALO),
            pl.ds(HALO + W, HALO),
        )

    def unpacked_halo(k):
        lf, rt = sides_in[k, 0], sides_in[k, 1]
        re = jnp.where(low, rt, lf)
        im = pltpu.roll(jnp.where(low, lf, rt), HALO, 1)
        return re, im

    def ar_start(a, value):
        ar_src[a, 0] = value
        ar_z[a, me_n] = value

        def send(i, c):
            pltpu.make_async_remote_copy(
                src_ref=ar_src.at[a, 0],
                dst_ref=ar_z.at[a, me_n],
                send_sem=ar_send.at[a, 0],
                recv_sem=ar_recv.at[a, 0],
                device_id=dev(me_w, me_n + i),
                device_id_type=MESH,
            ).start()
            return c

        lax.fori_loop(1, narrow, send, 0)

    def ar_middle(a):
        some = ar_z.at[a, pl.ds(0, narrow - 1)]
        pltpu.make_async_copy(some, some, ar_recv.at[a, 0]).wait()
        value = jnp.sum(ar_z[a], axis=0)
        ar_src[a, 1] = value
        ar_w[a, me_w] = value

        def send(i, c):
            pltpu.make_async_remote_copy(
                src_ref=ar_src.at[a, 1],
                dst_ref=ar_w.at[a, me_w],
                send_sem=ar_send.at[a, 1],
                recv_sem=ar_recv.at[a, 1],
                device_id=dev(me_w + i, me_n),
                device_id_type=MESH,
            ).start()
            return c

        lax.fori_loop(1, wide, send, 0)

    def ar_finish(a):
        some = ar_w.at[a, pl.ds(0, wide - 1)]
        pltpu.make_async_copy(some, some, ar_recv.at[a, 1]).wait()
        total = jnp.sum(ar_w[a], axis=0)
        total = jnp.sum(total, axis=1, keepdims=True)
        return total[0:1], total[1:2]

    def ar_drain(a):
        some = ar_z.at[a, pl.ds(0, narrow - 1)]
        pltpu.make_async_copy(some, some, ar_send.at[a, 0]).wait()
        some = ar_w.at[a, pl.ds(0, wide - 1)]
        pltpu.make_async_copy(some, some, ar_send.at[a, 1]).wait()

    def squares(x):
        s = jnp.sum(x * x, axis=0, keepdims=True)
        return s[:, :LANES] + s[:, LANES:]

    count = counts[0, 0]
    halves = (slice(0, LANES), slice(LANES, W))

    def load_patch(step, f):
        o0, o1 = offs[0, 0, 0, f], offs[0, 0, 1, f]
        own = (lane + o1 >= 0) & (lane + o1 < LANES)
        shift = lax.rem(LANES - o1, LANES)
        window = pl.ds(HALO + o0, W)
        for q in range(2):
            strip = side[step, q, window, :]
            a = jnp.where(lane < o1, strip, ext[step, q, 0, window, :])
            b = jnp.where(lane >= LANES + o1, strip, ext[step, q, 1, window, :])
            a, b = pltpu.roll(a, shift, 1), pltpu.roll(b, shift, 1)
            patch[q, :, :LANES] = jnp.where(own, a, b)
            patch[q, :, LANES:] = jnp.where(own, b, a)

    def exit_wave(m):
        pr, pi = probe[m, 0].astype(F32), probe[m, 1].astype(F32)
        xr, xi = patch[0], patch[1]
        waves[m, :W] = (pr * xr - pi * xi).astype(BF16)
        waves[m, W:] = (pr * xi + pi * xr).astype(BF16)

    def weigh(step, f, m):
        p = proj[step, f]
        waves[m, :W] = (weight[f, m, 0].astype(F32) * p).astype(BF16)
        waves[m, W:] = (weight[f, m, 1].astype(F32) * p).astype(BF16)

    def transform(left_table, right_table, refill):
        for m in range(MODES):
            part = jnp.dot(tab[left_table], waves[m], preferred_element_type=F32).astype(BF16)
            parts[m * W : (m + 1) * W, :W] = part[:W]
            parts[m * W : (m + 1) * W, W:] = part[W:]
            refill(m)
        return jnp.dot(parts[...], tab[right_table], preferred_element_type=F32)

    def forward(step):
        load_patch(step, 0)
        for m in range(MODES):
            exit_wave(m)

        def frame(f, total):
            load_patch(step, jnp.minimum(f + 1, FCAP - 1))
            far = transform(0, 1, exit_wave)
            p = jnp.zeros((W, W), F32)
            for m in range(MODES):
                one = far[m * W : (m + 1) * W]
                p += weight[f, m, 0].astype(F32) * one[:, :W] + weight[f, m, 1].astype(F32) * one[:, W:]
            p = p * (f < count).astype(F32)
            proj[step, f] = p
            return total + squares(p)

        return lax.fori_loop(0, FCAP, frame, jnp.zeros((1, LANES), F32))

    def spread(step, f):
        o0, o1 = offs[0, 0, 0, f], offs[0, 0, 1, f]
        own = (lane - o1 >= 0) & (lane - o1 < LANES)
        shift = lax.rem(LANES + o1, LANES)
        window = pl.ds(HALO - o0, EXT)
        to_right, to_left = lane < o1, lane >= LANES + o1
        for q in range(2):
            a = pltpu.roll(patch[q, :, :LANES], shift, 1)
            b = pltpu.roll(patch[q, :, LANES:], shift, 1)
            pad[q, 0, 2 * HALO : 2 * HALO + W, :] = jnp.where(own, a, b)
            pad[q, 1, 2 * HALO : 2 * HALO + W, :] = jnp.where(own, b, a)
            a, b = pad[q, 0, window, :], pad[q, 1, window, :]
            acc[step, q, :, :LANES] += jnp.where(to_right, 0.0, a)
            acc[step, q, :, LANES:] += jnp.where(to_left, 0.0, b)
            acc_side[q] += jnp.where(to_right, a, jnp.where(to_left, b, 0.0))

    def backward(step):
        for m in range(MODES):
            weigh(step, 0, m)
        patch[...] = jnp.zeros_like(patch)

        def frame(f, c):
            spread(step, jnp.maximum(f - 1, 0))
            near = transform(1, 0, functools.partial(weigh, step, jnp.minimum(f + 1, FCAP - 1)))
            re, im = jnp.zeros((W, W), F32), jnp.zeros((W, W), F32)
            for m in range(MODES):
                pr, pi = probe[m, 0].astype(F32), probe[m, 1].astype(F32)
                nr, ni = near[m * W : (m + 1) * W, :W], near[m * W : (m + 1) * W, W:]
                re += pr * nr + pi * ni
                im += pr * ni - pi * nr
            patch[0], patch[1] = re, im
            return c

        lax.fori_loop(0, FCAP, frame, 0)
        ar_middle(2 * step)
        spread(step, FCAP - 1)

    def pack_fold(k):
        re, im = acc_side[0], pltpu.roll(acc_side[1], HALO, 1)
        packs[k, 1] = jnp.where(low, re, im)
        packs[k, 0] = jnp.where(low, im, re)

    def own_image(step):
        for q in range(2):
            for h in range(2):
                own = acc[step, q, HALO : HALO + W, halves[h]]
                image[q, :, halves[h]] = own + DAMPING * ext[step, q, h, HALO : HALO + W, :]

    def fold_in(k):
        for q in range(2):
            image[q, :HALO, :] += rows_in[k, 0, q]
            image[q, W - HALO :, :] += rows_in[k, 1, q]
        lf, rt = sides_in[k, 0], sides_in[k, 1]
        for rows, piece in (
            (slice(0, W), slice(HALO, HALO + W)),
            (slice(0, HALO), slice(0, HALO)),
            (slice(W - HALO, W), slice(HALO + W, EXT)),
        ):
            l, r = lf[piece], rt[piece]
            image[0, rows, :LANES] += jnp.where(low, l, 0.0)
            image[0, rows, LANES:] += jnp.where(low, 0.0, r)
            image[1, rows, :LANES] += jnp.where(low, pltpu.roll(l, HALO, 1), 0.0)
            image[1, rows, LANES:] += jnp.where(low, 0.0, pltpu.roll(r, HALO, 1))

    loads[0].wait()
    pack_halo(grad, 0)
    pl.semaphore_wait(barrier, wide + narrow + 2)
    x0 = halo_exchange(0, grad)

    def no_rows(e, rows):
        rows_in[:, e] = jnp.zeros_like(rows_in[:, e])
        sides_in[:, :, rows, :] = jnp.zeros_like(sides_in[:, :, rows, :])

    def no_columns(e):
        sides_in[:, e] = jnp.zeros_like(sides_in[:, e])

    pl.when(~has_up)(lambda: no_rows(0, slice(0, HALO)))
    pl.when(~has_down)(lambda: no_rows(1, slice(HALO + W, EXT)))
    pl.when(~has_left)(lambda: no_columns(0))
    pl.when(~has_right)(lambda: no_columns(1))
    pad[...] = jnp.zeros_like(pad)
    acc[...] = jnp.zeros_like(acc)
    acc_side[...] = jnp.zeros_like(acc_side)
    norm = jnp.zeros((1, LANES), F32)
    for q in range(2):
        for h in range(2):
            ext[0, q, h, HALO : HALO + W, :] = grad[q, :, halves[h]]
        norm += squares(grad[q])
    for load in loads[1:]:
        load.wait()

    receive(x0)
    ends = ((slice(0, HALO), 0), (slice(HALO + W, EXT), 1))
    for rows, e in ends:
        for q in range(2):
            for h in range(2):
                ext[0, q, h, rows, :] = rows_in[0, e, q, :, halves[h]]
    halo = unpacked_halo(0)
    for q in range(2):
        side[0, q] = halo[q]

    total = forward(0) + DAMPING * norm
    ar_start(0, jnp.concatenate([norm, total], axis=0))
    backward(0)
    pack_fold(1)
    x1 = fold_exchange(1, 0)
    own_image(0)
    acc_side[...] = jnp.zeros_like(acc_side)
    receive(x1)
    fold_in(1)
    pack_halo(image, 2)

    norm0, curvature = ar_finish(0)
    alpha0 = norm0 / curvature
    norm = jnp.zeros((1, LANES), F32)
    for q in range(2):
        for h in range(2):
            r = grad[q, :, halves[h]] - alpha0 * image[q, :, halves[h]]
            ext[1, q, h, HALO : HALO + W, :] = r
            res_ref[q, :, halves[h]] = r
            norm += jnp.sum(r * r, axis=0, keepdims=True)
    ar_start(1, jnp.concatenate([norm, norm], axis=0))
    x2 = halo_exchange(2, image)
    ar_middle(1)
    receive(x2)
    halo = unpacked_halo(2)
    for q in range(2):
        side[1, q] = side[0, q] - alpha0 * halo[q]
        for rows, e in ends:
            for h in range(2):
                ext[1, q, h, rows, :] = ext[0, q, h, rows, :] - alpha0 * rows_in[2, e, q, :, halves[h]]

    forward(1)
    norm1, _ = ar_finish(1)
    beta = norm1 / norm0
    norm = jnp.zeros((1, LANES), F32)
    total = jnp.zeros((1, LANES), F32)
    for f in range(FCAP):
        p = proj[1, f] + beta * proj[0, f]
        proj[1, f] = p
        total += squares(p)
    for q in range(2):
        for h in range(2):
            d = ext[1, q, h, HALO : HALO + W, :] + beta * grad[q, :, halves[h]]
            ext[1, q, h, HALO : HALO + W, :] = d
            norm += jnp.sum(d * d, axis=0, keepdims=True)
    total += DAMPING * norm
    ar_start(2, jnp.concatenate([total, total], axis=0))
    backward(1)
    pack_fold(3)
    x3 = fold_exchange(3, 1)
    sent(x2)
    own_image(1)
    curvature, _ = ar_finish(2)
    alpha1 = norm1 / curvature
    for q in range(2):
        for h in range(2):
            sol_ref[q, :, halves[h]] = alpha0 * grad[q, :, halves[h]] + alpha1 * ext[1, q, h, HALO : HALO + W, :]
    receive(x3)
    fold_in(3)
    for q in range(2):
        res_ref[q] = res_ref[q] - alpha1 * image[q]

    sent(x0 + x1 + x3)
    for a in range(3):
        ar_drain(a)


def copy_kernel(a, b, x, y, buffers, in_sems, out_sems):
    pairs = [(a.at[0], x.at[0]), (a.at[1], x.at[1]), (b.at[0], y.at[0]), (b.at[1], y.at[1])]
    ins = [pltpu.make_async_copy(src, buffers.at[i], in_sems.at[i]) for i, (src, _) in enumerate(pairs)]
    outs = [pltpu.make_async_copy(buffers.at[i], dst, out_sems.at[i]) for i, (_, dst) in enumerate(pairs)]
    for copy in ins:
        copy.start()
    for i, copy in enumerate(outs):
        ins[i].wait()
        copy.start()
    for copy in outs:
        copy.wait()


def solution(mesh):
    wide, narrow = mesh.shape["wide"], mesh.shape["narrow"]
    tab = tables()
    tile = jax.ShapeDtypeStruct((2, W, W), F32)
    hbm = pl.BlockSpec(memory_space=pl.ANY)
    smem = pl.BlockSpec(memory_space=pltpu.SMEM)
    vmem = pl.BlockSpec(memory_space=pltpu.VMEM)

    def local(gradient, probe_modes, mode_weights, offsets, counts):
        results = pl.pallas_call(
            functools.partial(kernel, wide, narrow),
            out_shape=(tile, tile),
            in_specs=[smem, smem, hbm, hbm, hbm, hbm],
            out_specs=(vmem, vmem),
            scratch_shapes=[
                pltpu.VMEM((2, W, W), F32),
                pltpu.VMEM((2, 2 * W, 2 * W), BF16),
                pltpu.VMEM((MODES, 2, W, W), BF16),
                pltpu.VMEM((FCAP, MODES, 2, W, W), BF16),
                pltpu.VMEM((2, 2, 2, EXT, LANES), F32),
                pltpu.VMEM((2, 2, EXT, LANES), F32),
                pltpu.VMEM((2, 2, EXT, W), F32),
                pltpu.VMEM((2, EXT, LANES), F32),
                pltpu.VMEM((2, W, W), F32),
                pltpu.VMEM((4, 2, EXT, LANES), F32),
                pltpu.VMEM((4, 2, 2, HALO, W), F32),
                pltpu.VMEM((4, 2, EXT, LANES), F32),
                pltpu.VMEM((2, W, W), F32),
                pltpu.VMEM((MODES, 2 * W, W), BF16),
                pltpu.VMEM((MODES * W, 2 * W), BF16),
                pltpu.VMEM((2, FCAP, W, W), F32),
                pltpu.VMEM((2, 2, EXT + 2 * HALO, LANES), F32),
                pltpu.VMEM((3, 2, 2, LANES), F32),
                pltpu.VMEM((3, narrow, 2, LANES), F32),
                pltpu.VMEM((3, wide, 2, LANES), F32),
                pltpu.SemaphoreType.DMA((4,)),
                pltpu.SemaphoreType.DMA((4, 8)),
                pltpu.SemaphoreType.DMA((4, 8)),
                pltpu.SemaphoreType.DMA((3, 2)),
                pltpu.SemaphoreType.DMA((3, 2)),
            ],
            compiler_params=pltpu.CompilerParams(
                collective_id=0, has_side_effects=True, vmem_limit_bytes=60 * 1024 * 1024
            ),
        )(jnp.swapaxes(offsets, 2, 3), counts, jnp.asarray(tab), gradient, probe_modes, mode_weights)
        return pl.pallas_call(
            copy_kernel,
            out_shape=(tile, tile),
            in_specs=[hbm, hbm],
            out_specs=(hbm, hbm),
            scratch_shapes=[
                pltpu.VMEM((4, W, W), F32),
                pltpu.SemaphoreType.DMA((4,)),
                pltpu.SemaphoreType.DMA((4,)),
            ],
            compiler_params=pltpu.CompilerParams(vmem_limit_bytes=60 * 1024 * 1024),
        )(*results)

    spec = P(None, "wide", "narrow")
    return jax.shard_map(
        local,
        mesh=mesh,
        in_specs=(
            spec,
            P(),
            P("wide", "narrow", None, None, None, None, None),
            P("wide", "narrow", None, None),
            P("wide", "narrow"),
        ),
        out_specs=(spec, spec),
        check_vma=False,
    )
```

```python
import functools
import math

import jax
import jax.numpy as jnp
import numpy as np
from jax import lax
from jax.experimental import pallas as pl
from jax.experimental.pallas import tpu as pltpu
from jax.sharding import PartitionSpec as P

W = 256
MODES = 4
FCAP = 3
HALO = 64
EXT = W + 2 * HALO
LANES = 128
DAMPING = 0.5
MESH = pl.DeviceIdType.MESH
F32 = jnp.float32
BF16 = jnp.bfloat16


def tables():
    counter = np.arange(W)
    angles = (counter[:, None] * counter[None, :] % W) * (2.0 * math.pi / W)
    re = np.cos(angles) / math.sqrt(W)
    s = np.sin(angles) / math.sqrt(W)
    ahead = np.block([[re, s], [-s, re]])
    back = np.block([[re, -s], [s, re]])
    return np.stack([ahead, back]).astype(jnp.bfloat16)


def kernel(
    wide,
    narrow,
    offs,
    counts,
    tab_hbm,
    grad_hbm,
    probe_hbm,
    weight_hbm,
    sol_hbm,
    res_hbm,
    sol_ref,
    res_ref,
    grad,
    tab,
    probe,
    weight,
    ext,
    side,
    acc,
    acc_side,
    image,
    packs,
    rows_in,
    sides_in,
    patch,
    waves,
    parts,
    proj,
    pad,
    ar_src,
    ar_z,
    ar_w,
    load_sems,
    x_send,
    x_recv,
    ar_send,
    ar_recv,
):
    me_w, me_n = lax.axis_index("wide"), lax.axis_index("narrow")

    def dev(w, n):
        return (lax.rem(w, wide), lax.rem(n, narrow))

    up, down = me_w + wide - 1, me_w + 1
    left, right = me_n + narrow - 1, me_n + 1

    has_up, has_down = me_w > 0, me_w < wide - 1
    has_left, has_right = me_n > 0, me_n < narrow - 1

    loads = [
        pltpu.make_async_copy(grad_hbm, grad, load_sems.at[0]),
        pltpu.make_async_copy(tab_hbm, tab, load_sems.at[1]),
        pltpu.make_async_copy(probe_hbm, probe, load_sems.at[2]),
        pltpu.make_async_copy(weight_hbm.at[0, 0], weight, load_sems.at[3]),
    ]
    for load in loads:
        load.start()

    barrier = pltpu.get_barrier_semaphore()

    def greet_w(i, c):
        pl.semaphore_signal(barrier, inc=1, device_id=dev(me_w + i, me_n), device_id_type=MESH)
        return c

    def greet_n(i, c):
        pl.semaphore_signal(barrier, inc=1, device_id=dev(me_w, me_n + i), device_id_type=MESH)
        return c

    for w in (up, down):
        for n in (left, right):
            pl.semaphore_signal(barrier, inc=1, device_id=dev(w, n), device_id_type=MESH)
    lax.fori_loop(1, narrow, greet_n, 0)
    lax.fori_loop(1, wide, greet_w, 0)

    lane = lax.broadcasted_iota(jnp.int32, (1, LANES), 1)
    low = lane < HALO

    def pack_halo(src, k):
        re0, im0 = src[0, :, :LANES], src[1, :, :LANES]
        re1, im1 = src[0, :, LANES:], src[1, :, LANES:]
        packs[k, 0, HALO : HALO + W, :] = jnp.where(low, re0, pltpu.roll(im0, HALO, 1))
        packs[k, 1, HALO : HALO + W, :] = jnp.where(low, pltpu.roll(im1, HALO, 1), re1)

    def exchange(k, row_up, row_down, corner_up, corner_down):
        mid = pl.ds(HALO, W)
        first, last = pl.ds(0, HALO), pl.ds(HALO + W, HALO)
        plan = [
            (packs.at[k, 0, corner_up], sides_in.at[k, 1, last], (up, left), has_up & has_left, has_down & has_right),
            (packs.at[k, 1, corner_up], sides_in.at[k, 0, last], (up, right), has_up & has_right, has_down & has_left),
            (packs.at[k, 0, corner_down], sides_in.at[k, 1, first], (down, left), has_down & has_left, has_up & has_right),
            (packs.at[k, 1, corner_down], sides_in.at[k, 0, first], (down, right), has_down & has_right, has_up & has_left),
            (packs.at[k, 0, mid], sides_in.at[k, 1, mid], (me_w, left), has_left, has_right),
            (packs.at[k, 1, mid], sides_in.at[k, 0, mid], (me_w, right), has_right, has_left),
            (row_up, rows_in.at[k, 1], (up, me_n), has_up, has_down),
            (row_down, rows_in.at[k, 0], (down, me_n), has_down, has_up),
        ]
        copies = []
        for j, (src, dst, where, sends, receives) in enumerate(plan):
            copy = pltpu.make_async_remote_copy(
                src_ref=src,
                dst_ref=dst,
                send_sem=x_send.at[k, j],
                recv_sem=x_recv.at[k, j],
                device_id=dev(*where),
                device_id_type=MESH,
            )
            pl.when(sends)(copy.start)
            copies.append((copy, sends, receives))
        return copies

    def receive(copies):
        for copy, _, receives in copies:
            pl.when(receives)(copy.wait_recv)

    def sent(copies):
        for copy, sends, _ in copies:
            pl.when(sends)(copy.wait_send)

    def halo_exchange(k, src):
        return exchange(
            k,
            src.at[:, pl.ds(0, HALO)],
            src.at[:, pl.ds(W - HALO, HALO)],
            pl.ds(HALO, HALO),
            pl.ds(W, HALO),
        )

    def fold_exchange(k, step):
        return exchange(
            k,
            acc.at[step, :, pl.ds(0, HALO)],
            acc.at[step, :, pl.ds(HALO + W, HALO)],
            pl.ds(0, HALO),
            pl.ds(HALO + W, HALO),
        )

    def unpacked_halo(k):
        lf, rt = sides_in[k, 0], sides_in[k, 1]
        re = jnp.where(low, rt, lf)
        im = pltpu.roll(jnp.where(low, lf, rt), HALO, 1)
        return re, im

    def ar_start(a, value):
        ar_src[a, 0] = value
        ar_z[a, me_n] = value

        def send(i, c):
            pltpu.make_async_remote_copy(
                src_ref=ar_src.at[a, 0],
                dst_ref=ar_z.at[a, me_n],
                send_sem=ar_send.at[a, 0],
                recv_sem=ar_recv.at[a, 0],
                device_id=dev(me_w, me_n + i),
                device_id_type=MESH,
            ).start()
            return c

        lax.fori_loop(1, narrow, send, 0)

    def ar_middle(a):
        some = ar_z.at[a, pl.ds(0, narrow - 1)]
        pltpu.make_async_copy(some, some, ar_recv.at[a, 0]).wait()
        value = jnp.sum(ar_z[a], axis=0)
        ar_src[a, 1] = value
        ar_w[a, me_w] = value

        def send(i, c):
            pltpu.make_async_remote_copy(
                src_ref=ar_src.at[a, 1],
                dst_ref=ar_w.at[a, me_w],
                send_sem=ar_send.at[a, 1],
                recv_sem=ar_recv.at[a, 1],
                device_id=dev(me_w + i, me_n),
                device_id_type=MESH,
            ).start()
            return c

        lax.fori_loop(1, wide, send, 0)

    def ar_finish(a):
        some = ar_w.at[a, pl.ds(0, wide - 1)]
        pltpu.make_async_copy(some, some, ar_recv.at[a, 1]).wait()
        total = jnp.sum(ar_w[a], axis=0)
        total = jnp.sum(total, axis=1, keepdims=True)
        return total[0:1], total[1:2]

    def ar_drain(a):
        some = ar_z.at[a, pl.ds(0, narrow - 1)]
        pltpu.make_async_copy(some, some, ar_send.at[a, 0]).wait()
        some = ar_w.at[a, pl.ds(0, wide - 1)]
        pltpu.make_async_copy(some, some, ar_send.at[a, 1]).wait()

    def squares(x):
        s = jnp.sum(x * x, axis=0, keepdims=True)
        return s[:, :LANES] + s[:, LANES:]

    count = counts[0, 0]
    halves = (slice(0, LANES), slice(LANES, W))

    def load_patch(step, f):
        o0, o1 = offs[0, 0, 0, f], offs[0, 0, 1, f]
        own = (lane + o1 >= 0) & (lane + o1 < LANES)
        shift = lax.rem(LANES - o1, LANES)
        window = pl.ds(HALO + o0, W)
        for q in range(2):
            strip = side[step, q, window, :]
            a = jnp.where(lane < o1, strip, ext[step, q, 0, window, :])
            b = jnp.where(lane >= LANES + o1, strip, ext[step, q, 1, window, :])
            a, b = pltpu.roll(a, shift, 1), pltpu.roll(b, shift, 1)
            patch[q, :, :LANES] = jnp.where(own, a, b)
            patch[q, :, LANES:] = jnp.where(own, b, a)

    def exit_wave(m):
        pr, pi = probe[m, 0].astype(F32), probe[m, 1].astype(F32)
        xr, xi = patch[0], patch[1]
        waves[m, :W] = (pr * xr - pi * xi).astype(BF16)
        waves[m, W:] = (pr * xi + pi * xr).astype(BF16)

    def weigh(step, f, m):
        p = proj[step, f]
        waves[m, :W] = (weight[f, m, 0].astype(F32) * p).astype(BF16)
        waves[m, W:] = (weight[f, m, 1].astype(F32) * p).astype(BF16)

    def transform(left_table, right_table, refill):
        for m in range(MODES):
            part = jnp.dot(tab[left_table], waves[m], preferred_element_type=F32).astype(BF16)
            parts[m * W : (m + 1) * W, :W] = part[:W]
            parts[m * W : (m + 1) * W, W:] = part[W:]
            refill(m)
        return jnp.dot(parts[...], tab[right_table], preferred_element_type=F32)

    def forward(step):
        load_patch(step, 0)
        for m in range(MODES):
            exit_wave(m)

        def frame(f, total):
            load_patch(step, jnp.minimum(f + 1, FCAP - 1))
            far = transform(0, 1, exit_wave)
            p = jnp.zeros((W, W), F32)
            for m in range(MODES):
                one = far[m * W : (m + 1) * W]
                p += weight[f, m, 0].astype(F32) * one[:, :W] + weight[f, m, 1].astype(F32) * one[:, W:]
            p = p * (f < count).astype(F32)
            proj[step, f] = p
            return total + squares(p)

        return lax.fori_loop(0, FCAP, frame, jnp.zeros((1, LANES), F32))

    def spread(step, f):
        o0, o1 = offs[0, 0, 0, f], offs[0, 0, 1, f]
        own = (lane - o1 >= 0) & (lane - o1 < LANES)
        shift = lax.rem(LANES + o1, LANES)
        window = pl.ds(HALO - o0, EXT)
        to_right, to_left = lane < o1, lane >= LANES + o1
        for q in range(2):
            a = pltpu.roll(patch[q, :, :LANES], shift, 1)
            b = pltpu.roll(patch[q, :, LANES:], shift, 1)
            pad[q, 0, 2 * HALO : 2 * HALO + W, :] = jnp.where(own, a, b)
            pad[q, 1, 2 * HALO : 2 * HALO + W, :] = jnp.where(own, b, a)
            a, b = pad[q, 0, window, :], pad[q, 1, window, :]
            acc[step, q, :, :LANES] += jnp.where(to_right, 0.0, a)
            acc[step, q, :, LANES:] += jnp.where(to_left, 0.0, b)
            acc_side[q] += jnp.where(to_right, a, jnp.where(to_left, b, 0.0))

    def backward(step):
        for m in range(MODES):
            weigh(step, 0, m)
        patch[...] = jnp.zeros_like(patch)

        def frame(f, c):
            spread(step, jnp.maximum(f - 1, 0))
            near = transform(1, 0, functools.partial(weigh, step, jnp.minimum(f + 1, FCAP - 1)))
            re, im = jnp.zeros((W, W), F32), jnp.zeros((W, W), F32)
            for m in range(MODES):
                pr, pi = probe[m, 0].astype(F32), probe[m, 1].astype(F32)
                nr, ni = near[m * W : (m + 1) * W, :W], near[m * W : (m + 1) * W, W:]
                re += pr * nr + pi * ni
                im += pr * ni - pi * nr
            patch[0], patch[1] = re, im
            return c

        lax.fori_loop(0, FCAP, frame, 0)
        ar_middle(2 * step)
        spread(step, FCAP - 1)

    def pack_fold(k):
        re, im = acc_side[0], pltpu.roll(acc_side[1], HALO, 1)
        packs[k, 1] = jnp.where(low, re, im)
        packs[k, 0] = jnp.where(low, im, re)

    def own_image(step):
        for q in range(2):
            for h in range(2):
                own = acc[step, q, HALO : HALO + W, halves[h]]
                image[q, :, halves[h]] = own + DAMPING * ext[step, q, h, HALO : HALO + W, :]

    def fold_in(k):
        for q in range(2):
            image[q, :HALO, :] += rows_in[k, 0, q]
            image[q, W - HALO :, :] += rows_in[k, 1, q]
        lf, rt = sides_in[k, 0], sides_in[k, 1]
        for rows, piece in (
            (slice(0, W), slice(HALO, HALO + W)),
            (slice(0, HALO), slice(0, HALO)),
            (slice(W - HALO, W), slice(HALO + W, EXT)),
        ):
            l, r = lf[piece], rt[piece]
            image[0, rows, :LANES] += jnp.where(low, l, 0.0)
            image[0, rows, LANES:] += jnp.where(low, 0.0, r)
            image[1, rows, :LANES] += jnp.where(low, pltpu.roll(l, HALO, 1), 0.0)
            image[1, rows, LANES:] += jnp.where(low, 0.0, pltpu.roll(r, HALO, 1))

    loads[0].wait()
    pack_halo(grad, 0)
    pl.semaphore_wait(barrier, wide + narrow + 2)
    x0 = halo_exchange(0, grad)

    def no_rows(e, rows):
        rows_in[:, e] = jnp.zeros_like(rows_in[:, e])
        sides_in[:, :, rows, :] = jnp.zeros_like(sides_in[:, :, rows, :])

    def no_columns(e):
        sides_in[:, e] = jnp.zeros_like(sides_in[:, e])

    pl.when(~has_up)(lambda: no_rows(0, slice(0, HALO)))
    pl.when(~has_down)(lambda: no_rows(1, slice(HALO + W, EXT)))
    pl.when(~has_left)(lambda: no_columns(0))
    pl.when(~has_right)(lambda: no_columns(1))
    pad[...] = jnp.zeros_like(pad)
    acc[...] = jnp.zeros_like(acc)
    acc_side[...] = jnp.zeros_like(acc_side)
    norm = jnp.zeros((1, LANES), F32)
    for q in range(2):
        for h in range(2):
            ext[0, q, h, HALO : HALO + W, :] = grad[q, :, halves[h]]
        norm += squares(grad[q])
    for load in loads[1:]:
        load.wait()

    receive(x0)
    ends = ((slice(0, HALO), 0), (slice(HALO + W, EXT), 1))
    for rows, e in ends:
        for q in range(2):
            for h in range(2):
                ext[0, q, h, rows, :] = rows_in[0, e, q, :, halves[h]]
    halo = unpacked_halo(0)
    for q in range(2):
        side[0, q] = halo[q]

    total = forward(0) + DAMPING * norm
    ar_start(0, jnp.concatenate([norm, total], axis=0))
    backward(0)
    pack_fold(1)
    x1 = fold_exchange(1, 0)
    own_image(0)
    acc_side[...] = jnp.zeros_like(acc_side)
    receive(x1)
    fold_in(1)
    pack_halo(image, 2)

    norm0, curvature = ar_finish(0)
    alpha0 = norm0 / curvature
    norm = jnp.zeros((1, LANES), F32)
    for q in range(2):
        for h in range(2):
            r = grad[q, :, halves[h]] - alpha0 * image[q, :, halves[h]]
            ext[1, q, h, HALO : HALO + W, :] = r
            res_ref[q, :, halves[h]] = r
            norm += jnp.sum(r * r, axis=0, keepdims=True)
    ar_start(1, jnp.concatenate([norm, norm], axis=0))
    x2 = halo_exchange(2, image)
    ar_middle(1)
    receive(x2)
    halo = unpacked_halo(2)
    for q in range(2):
        side[1, q] = side[0, q] - alpha0 * halo[q]
        for rows, e in ends:
            for h in range(2):
                ext[1, q, h, rows, :] = ext[0, q, h, rows, :] - alpha0 * rows_in[2, e, q, :, halves[h]]

    forward(1)
    norm1, _ = ar_finish(1)
    beta = norm1 / norm0
    norm = jnp.zeros((1, LANES), F32)
    total = jnp.zeros((1, LANES), F32)
    for f in range(FCAP):
        p = proj[1, f] + beta * proj[0, f]
        proj[1, f] = p
        total += squares(p)
    for q in range(2):
        for h in range(2):
            d = ext[1, q, h, HALO : HALO + W, :] + beta * grad[q, :, halves[h]]
            ext[1, q, h, HALO : HALO + W, :] = d
            norm += jnp.sum(d * d, axis=0, keepdims=True)
    total += DAMPING * norm
    ar_start(2, jnp.concatenate([total, total], axis=0))
    backward(1)
    pack_fold(3)
    x3 = fold_exchange(3, 1)
    sent(x2)
    own_image(1)
    curvature, _ = ar_finish(2)
    alpha1 = norm1 / curvature
    for q in range(2):
        for h in range(2):
            sol_ref[q, :, halves[h]] = alpha0 * grad[q, :, halves[h]] + alpha1 * ext[1, q, h, HALO : HALO + W, :]
    stores = [pltpu.make_async_copy(sol_ref, sol_hbm, load_sems.at[4])]
    stores[0].start()
    receive(x3)
    fold_in(3)
    for q in range(2):
        res_ref[q] = res_ref[q] - alpha1 * image[q]
        stores.append(pltpu.make_async_copy(res_ref.at[q], res_hbm.at[q], load_sems.at[5 + q]))
        stores[-1].start()

    sent(x0 + x1 + x3)
    for store in stores:
        store.wait()
    for a in range(3):
        ar_drain(a)


def copy_kernel(a, b, x, y, buffers, in_sems, out_sems):
    pairs = [(a.at[0], x.at[0]), (a.at[1], x.at[1]), (b.at[0], y.at[0]), (b.at[1], y.at[1])]
    ins = [pltpu.make_async_copy(src, buffers.at[i], in_sems.at[i]) for i, (src, _) in enumerate(pairs)]
    outs = [pltpu.make_async_copy(buffers.at[i], dst, out_sems.at[i]) for i, (_, dst) in enumerate(pairs)]
    for copy in ins:
        copy.start()
    for i, copy in enumerate(outs):
        ins[i].wait()
        copy.start()
    for copy in outs:
        copy.wait()


def solution(mesh):
    wide, narrow = mesh.shape["wide"], mesh.shape["narrow"]
    tab = tables()
    tile = jax.ShapeDtypeStruct((2, W, W), F32)
    hbm = pl.BlockSpec(memory_space=pl.ANY)
    smem = pl.BlockSpec(memory_space=pltpu.SMEM)

    def local(gradient, probe_modes, mode_weights, offsets, counts):
        results = pl.pallas_call(
            functools.partial(kernel, wide, narrow),
            out_shape=(tile, tile),
            in_specs=[smem, smem, hbm, hbm, hbm, hbm],
            out_specs=(hbm, hbm),
            scratch_shapes=[
                pltpu.VMEM((2, W, W), F32),
                pltpu.VMEM((2, W, W), F32),
                pltpu.VMEM((2, W, W), F32),
                pltpu.VMEM((2, 2 * W, 2 * W), BF16),
                pltpu.VMEM((MODES, 2, W, W), BF16),
                pltpu.VMEM((FCAP, MODES, 2, W, W), BF16),
                pltpu.VMEM((2, 2, 2, EXT, LANES), F32),
                pltpu.VMEM((2, 2, EXT, LANES), F32),
                pltpu.VMEM((2, 2, EXT, W), F32),
                pltpu.VMEM((2, EXT, LANES), F32),
                pltpu.VMEM((2, W, W), F32),
                pltpu.VMEM((4, 2, EXT, LANES), F32),
                pltpu.VMEM((4, 2, 2, HALO, W), F32),
                pltpu.VMEM((4, 2, EXT, LANES), F32),
                pltpu.VMEM((2, W, W), F32),
                pltpu.VMEM((MODES, 2 * W, W), BF16),
                pltpu.VMEM((MODES * W, 2 * W), BF16),
                pltpu.VMEM((2, FCAP, W, W), F32),
                pltpu.VMEM((2, 2, EXT + 2 * HALO, LANES), F32),
                pltpu.VMEM((3, 2, 2, LANES), F32),
                pltpu.VMEM((3, narrow, 2, LANES), F32),
                pltpu.VMEM((3, wide, 2, LANES), F32),
                pltpu.SemaphoreType.DMA((7,)),
                pltpu.SemaphoreType.DMA((4, 8)),
                pltpu.SemaphoreType.DMA((4, 8)),
                pltpu.SemaphoreType.DMA((3, 2)),
                pltpu.SemaphoreType.DMA((3, 2)),
            ],
            compiler_params=pltpu.CompilerParams(
                collective_id=0, has_side_effects=True, vmem_limit_bytes=60 * 1024 * 1024
            ),
        )(jnp.swapaxes(offsets, 2, 3), counts, jnp.asarray(tab), gradient, probe_modes, mode_weights)
        return pl.pallas_call(
            copy_kernel,
            out_shape=(tile, tile),
            in_specs=[hbm, hbm],
            out_specs=(hbm, hbm),
            scratch_shapes=[
                pltpu.VMEM((4, W, W), F32),
                pltpu.SemaphoreType.DMA((4,)),
                pltpu.SemaphoreType.DMA((4,)),
            ],
            compiler_params=pltpu.CompilerParams(vmem_limit_bytes=60 * 1024 * 1024),
        )(*results)

    spec = P(None, "wide", "narrow")
    return jax.shard_map(
        local,
        mesh=mesh,
        in_specs=(
            spec,
            P(),
            P("wide", "narrow", None, None, None, None, None),
            P("wide", "narrow", None, None),
            P("wide", "narrow"),
        ),
        out_specs=(spec, spec),
        check_vma=False,
    )
```
